128 devices in a mesh: pairs: 64 (over y, x, z), aux: 2 (over core).
Axes of the slice: x: 4, y: 4, z: 4, core: 2. Of those that a mesh axis runs over, the one named last changes fastest.
Arguments:
- densities: bfloat16 [16, 49152], P(None, 'pairs'), may hold values from -6 to 6
- tensor: bfloat16 [49152, 20480], P('pairs', 'aux'), may hold values from -0.078125 to 0.078125
- metric: bfloat16 [20480, 20480], P('aux', 'pairs'), may hold values from -0.0390625 to 0.0390625
- row_count: int32 [64], P('pairs'), may hold values from 1 to 768, 30720 in all
Outputs:
- coulomb: bfloat16 [16, 49152], P('aux', 'pairs')
The draws below stay inside these ranges and needn't reach their ends.
Inputs may be any that keep to these rules, and one draw needn't show every extreme that they name: The first row_count[b] rows of pair block b are live; some block has all 768 rows live.
All inputs are finite; a program needn't handle non-finite values.
Results may differ from the reference program's by a relative error of at most 0.0057.
Values may be sent and summed in bfloat16 or wider, within the bound.
A program may use at most 64 MiB of HBM per device.

```python
import math
import jax
import jax.numpy as jnp
import numpy as np
from jax import lax

NAUX = 20480
K = 16
ROWS_DEV = 768
ROWS = 49152
N_PAIRS = 64


def with_spikes(entries, key, source, target, parts, factor):
    owner, partner = [(jnp.arange(entries.shape[position]) // (entries.shape[position] // parts)).reshape([-1 if axis == position else 1 for axis in range(entries.ndim)]) for position in (source, target)]
    chosen = jax.random.permutation(key, parts)[partner]
    strong = (owner == chosen) | (owner == (partner + parts // 2) % parts)
    return jnp.where(strong, factor * entries, entries)


def levels(rng, shape, cuts, smallest, high):
    loudness = 1.0
    for axis_at, blocks in cuts:
        heights = jax.random.uniform(jax.random.fold_in(jax.random.fold_in(rng, 6), axis_at), (blocks,), jnp.float32, smallest / len(cuts), high / len(cuts))
        loudness = loudness * jnp.repeat(jnp.exp(heights), shape[axis_at] // blocks).reshape((-1,) + (1,) * (len(shape) - 1 - axis_at))
    return loudness


def length_profile(count, total, limit, slope):
    loads = [(1 << 20) // math.isqrt(rank ** slope) + 1 for rank in range(2, count + 1)]
    spare, holding = total - limit - (count - 1), [1] * (count - 1)
    while spare > 0:
        free = [i for i in range(count - 1) if holding[i] < limit]
        mass, budget = sum([loads[i] for i in free]), spare
        for i in free:
            addition = min(limit - holding[i], max(1, budget * loads[i] // mass), spare)
            holding[i] = holding[i] + addition
            spare = spare - addition
    return np.array([limit] + holding)


def uneven_parts(rng, number_of, total, most, slope):
    if number_of == 2:
        one = jax.random.randint(rng, (), max(1, total - most), min(most, total - 1) + 1)
        return jnp.stack([one, total - one])
    tallies = jnp.asarray(length_profile(number_of, total, most, slope), jnp.int32)
    pairs = (number_of - 1) // 2
    donor, taker = tallies[1:1 + 2 * pairs:2], tallies[2:2 + 2 * pairs:2]
    margin = jnp.minimum(donor - 1, most - taker)
    passed = jax.random.randint(jax.random.fold_in(rng, 1), (pairs,), 0, 1 << 20) % (margin + 1)
    tallies = tallies.at[1:1 + 2 * pairs:2].set(donor - passed).at[2:2 + 2 * pairs:2].set(taker + passed)
    return tallies[jax.random.permutation(jax.random.fold_in(rng, 2), number_of)]


def scatter_about(own_key, dims, scale, limit, shards=(), kind=jnp.bfloat16):
    level = levels(own_key, dims, shards, -0.22, 0.18) if shards else 1.0
    entries = jax.random.normal(own_key, dims, jnp.float32) * scale * level
    return jnp.minimum(jnp.maximum(entries, -limit), limit).astype(kind)


def bell_draw_with(own_key, dims, scale, limit, shards, heavy, held_as=jnp.bfloat16):
    array = scale * jax.random.normal(own_key, dims, jnp.float32)
    if shards:
        array = array * levels(own_key, dims, shards, -0.22, 0.18)
    return jnp.clip(with_spikes(array, jax.random.fold_in(own_key, 3), *heavy), -limit, limit).astype(held_as)


def setup_inputs(seed: int = 0) -> dict:
    splits = jax.random.split(jax.random.key(seed), 5)
    return {
        "densities": scatter_about(splits[0], (K, ROWS), 1.0, 6.0, ((1, 64),)),
        "tensor": bell_draw_with(splits[1], (ROWS, NAUX), ROWS ** -0.5, 0.078125, ((0, 64), (1, 2)), (0, 1, 64, 4.0)),
        "metric": scatter_about(splits[2], (NAUX, NAUX), NAUX ** -0.5, 0.0390625, ((0, 2), (1, 64))),
        "row_count": uneven_parts(splits[3], N_PAIRS, ROWS_DEV * N_PAIRS * 5 // 8, ROWS_DEV, 2).astype(jnp.int32),
    }


def reference(densities, tensor, metric, row_count):
    blocks = tensor.reshape(N_PAIRS, ROWS_DEV, NAUX)
    dense_blocks = densities.reshape(K, N_PAIRS, ROWS_DEV).transpose(1, 0, 2)
    positions = jnp.arange(ROWS_DEV, dtype=jnp.int32)
    live = positions[None, :] < row_count[:, None].astype(jnp.int32)

    def add_block(total, items):
        block, dense, alive = items
        masked = jnp.where(alive[None, :], dense, jnp.zeros_like(dense))
        term = jnp.dot(masked.astype(jnp.float32), block.astype(jnp.float32), precision=lax.Precision.HIGHEST)
        return total + term, None

    fitted, _ = lax.scan(add_block, jnp.zeros((K, NAUX), jnp.float32), (blocks, dense_blocks, live))
    fitted = fitted.astype(jnp.bfloat16)
    metric_rows = metric.reshape(N_PAIRS, NAUX // N_PAIRS, NAUX)
    fitted_rows = fitted.reshape(K, N_PAIRS, NAUX // N_PAIRS).transpose(1, 0, 2)

    def add_metric(total, items):
        rows_here, fit_here = items
        term = jnp.dot(fit_here.astype(jnp.float32), rows_here.astype(jnp.float32), precision=lax.Precision.HIGHEST)
        return total + term, None

    solved, _ = lax.scan(add_metric, jnp.zeros((K, NAUX), jnp.float32), (metric_rows, fitted_rows))
    solved = solved.astype(jnp.bfloat16).astype(jnp.float32)

    def back_block(items):
        block, alive = items
        term = jnp.dot(solved, block.astype(jnp.float32).T, precision=lax.Precision.HIGHEST)
        return jnp.where(alive[None, :], term, jnp.zeros_like(term))

    result = lax.map(back_block, (blocks, live))
    return result.transpose(1, 0, 2).reshape(K, N_PAIRS * ROWS_DEV).astype(jnp.bfloat16)
```

```python
import functools

import jax
import jax.numpy as jnp
from jax import lax
from jax.experimental import pallas as pl
from jax.experimental.pallas import tpu as pltpu
from jax.sharding import PartitionSpec as P

MESH = pl.DeviceIdType.MESH
NT = (((1,), (1,)), ((), ()))
K, ROWS, AUX, COLS = 16, 768, 10240, 320
TILE = 128
CHUNKS = (2048, 2048, 2048, 2048, 1024, 1024)
STEPS = (2, 1, 3, 0)


def hops(step):
    return sum(min(d, 4 - d) for d in step)


OFFSETS = sorted(
    [(a, b, d) for a in STEPS for b in STEPS for d in STEPS if (a, b, d) != (0, 0, 0)],
    key=lambda step: -hops(step),
)


def tiles_of(ref, first, count):
    return jnp.concatenate([ref[first + i] for i in range(count)], axis=1)


def kernel(
    count_ref, dens_hbm, tensor_hbm, metric_hbm, out_ref,
    tv, mv, dv, fit, got, got_extra, fitted, part, solved, pieces, back, returned,
    load_d, load_t, load_m, rs_send, rs_recv, rs_recv_extra,
    ag_send, ag_recv, ag_recv_extra, c_send, c_recv, d_send, d_recv, e_send, e_recv,
):
    p, c = lax.axis_index("pairs"), lax.axis_index("aux")
    y, x, z = p // 16, (p // 4) % 4, p % 4
    group = p // 4
    has_extra = z == (x + y) % 4
    owner = p // 32

    def chip(step):
        return ((y + step[0]) % 4 * 4 + (x + step[1]) % 4) * 4 + (z + step[2]) % 4

    load_dens = pltpu.make_async_copy(dens_hbm, dv, load_d)
    load_dens.start()
    loads, at = [], 0
    for i, width in enumerate(CHUNKS):
        piece = pltpu.make_async_copy(
            tensor_hbm.at[:, pl.ds(at, width)], tv.at[:, pl.ds(at, width)], load_t.at[i]
        )
        piece.start()
        loads.append((piece, at, width))
        at += width

    barrier = pltpu.get_barrier_semaphore()
    for step in OFFSETS:
        pl.semaphore_signal(barrier, inc=1, device_id=(chip(step), c), device_id_type=MESH)
    pl.semaphore_signal(barrier, inc=1, device_id=(p, 1 - c), device_id_type=MESH)

    load_dens.wait()
    live = lax.broadcasted_iota(jnp.int32, (K, ROWS), 1) < count_ref[0]
    masked = jnp.where(live, dv[...], jnp.zeros((K, ROWS), jnp.bfloat16))
    for piece, at, width in loads:
        piece.wait()
        term = jnp.dot(masked, tv[:, at : at + width], preferred_element_type=jnp.float32)
        term = term.astype(jnp.bfloat16)
        for i in range(width // TILE):
            fit[at // TILE + i] = term[:, i * TILE : (i + 1) * TILE]

    load_metric = pltpu.make_async_copy(metric_hbm, mv, load_m)
    load_metric.start()
    pl.semaphore_wait(barrier, len(OFFSETS) + 1)

    for step in OFFSETS:
        q = chip(step)
        pltpu.make_async_remote_copy(
            fit.at[q], got.at[p], rs_send, rs_recv, device_id=(q, c), device_id_type=MESH
        ).start()

        @pl.when((q % 4) == (q // 16 + (q // 4) % 4) % 4)
        def _():
            pltpu.make_async_remote_copy(
                fit.at[64 + q // 4], got_extra.at[p], rs_send, rs_recv_extra,
                device_id=(q, c), device_id_type=MESH,
            ).start()

    got[p] = fit[p]
    pltpu.make_async_copy(got.at[pl.ds(0, 63)], got.at[pl.ds(0, 63)], rs_recv).wait()
    total = jnp.sum(got[...].astype(jnp.float32), axis=0)
    fitted[p] = total.astype(jnp.bfloat16)
    for step in OFFSETS:
        pltpu.make_async_remote_copy(
            fitted.at[p], fitted.at[p], ag_send, ag_recv.at[(4 - step[0]) % 4],
            device_id=(chip(step), c), device_id_type=MESH,
        ).start()

    @pl.when(has_extra)
    def _():
        got_extra[p] = fit[64 + group]
        pltpu.make_async_copy(
            got_extra.at[pl.ds(0, 63)], got_extra.at[pl.ds(0, 63)], rs_recv_extra
        ).wait()
        total = jnp.sum(got_extra[...].astype(jnp.float32), axis=0)
        fitted[64 + group] = total.astype(jnp.bfloat16)
        for step in OFFSETS:
            pltpu.make_async_remote_copy(
                fitted.at[64 + group], fitted.at[64 + group], ag_send,
                ag_recv_extra.at[(4 - step[0]) % 4],
                device_id=(chip(step), c), device_id_type=MESH,
            ).start()

    load_metric.wait()
    half = jnp.zeros((K, COLS), jnp.float32)
    for dy in STEPS:
        plane = (y + dy) % 4
        mains = 16 if dy else 15
        pltpu.make_async_copy(
            fitted.at[pl.ds(0, mains)], fitted.at[pl.ds(0, mains)], ag_recv.at[dy]
        ).wait()
        if dy:
            pltpu.make_async_copy(
                fitted.at[pl.ds(64, 4)], fitted.at[pl.ds(64, 4)], ag_recv_extra.at[dy]
            ).wait()
        else:
            @pl.when(has_extra)
            def _():
                pltpu.make_async_copy(
                    fitted.at[pl.ds(64, 3)], fitted.at[pl.ds(64, 3)], ag_recv_extra.at[0]
                ).wait()

            @pl.when(jnp.logical_not(has_extra))
            def _():
                pltpu.make_async_copy(
                    fitted.at[pl.ds(64, 4)], fitted.at[pl.ds(64, 4)], ag_recv_extra.at[0]
                ).wait()

        for first, many in ((plane * 16, 16), (64 + plane * 4, 4)):
            columns = pl.ds(pl.multiple_of(first * TILE, TILE), many * TILE)
            half += lax.dot_general(
                tiles_of(fitted, first, many), mv[:, columns], NT,
                preferred_element_type=jnp.float32,
            )

    send_half = pltpu.make_async_remote_copy(
        part.at[0], part.at[1], c_send, c_recv, device_id=(p, 1 - c), device_id_type=MESH
    )

    @pl.when(c != owner)
    def _():
        part[0] = half
        send_half.start()
        send_half.wait_send()

    @pl.when(c == owner)
    def _():
        send_half.wait_recv()
        whole = (half + part[1]).astype(jnp.bfloat16)
        blank = jnp.zeros((K, TILE // 2), jnp.bfloat16)
        low = jnp.concatenate([whole, blank], axis=1)
        high = jnp.concatenate([blank, whole], axis=1)
        placed = jnp.where(jnp.full(low.shape, p % 2, jnp.int32) == 0, low, high)
        mine = p - 32 * owner
        for i in range(3):
            pieces[mine, i] = placed[:, i * TILE : (i + 1) * TILE]
        for step in OFFSETS:
            pltpu.make_async_remote_copy(
                pieces.at[mine], pieces.at[mine], d_send, d_recv.at[(4 - step[1]) % 4],
                device_id=(chip(step), c), device_id_type=MESH,
            ).start()

    total = jnp.zeros((K, ROWS), jnp.float32)
    for dx in STEPS:
        column = (x + dx) % 4
        if dx:
            pltpu.make_async_copy(
                pieces.at[pl.ds(0, 8)], pieces.at[pl.ds(0, 8)], d_recv.at[dx]
            ).wait()
        else:
            for here, many in ((True, 7), (False, 8)):
                @pl.when((c == owner) == here)
                def _():
                    pltpu.make_async_copy(
                        pieces.at[pl.ds(0, many)], pieces.at[pl.ds(0, many)], d_recv.at[0]
                    ).wait()

        for plane in range(2):
            first = plane * 16 + column * 4
            row = []
            for j in (0, 2):
                row += [
                    pieces[first + j, 0],
                    pieces[first + j, 1],
                    pieces[first + j, 2] + pieces[first + j + 1, 0],
                    pieces[first + j + 1, 1],
                    pieces[first + j + 1, 2],
                ]
            columns = pl.ds(pl.multiple_of(first * COLS, TILE), 4 * COLS)
            total += lax.dot_general(
                jnp.concatenate(row, axis=1), tv[:, columns], NT,
                preferred_element_type=jnp.float32,
            )

    back[0] = total[0:8]
    back[1] = total[8:16]
    swap = pltpu.make_async_remote_copy(
        back.at[1 - c], returned, e_send, e_recv, device_id=(p, 1 - c), device_id_type=MESH
    )
    swap.start()
    swap.wait_recv()
    result = back[c] + returned[...]
    alive = lax.broadcasted_iota(jnp.int32, (8, ROWS), 1) < count_ref[0]
    out_ref[...] = jnp.where(alive, result, jnp.zeros_like(result)).astype(jnp.bfloat16)

    swap.wait_send()
    pltpu.make_async_copy(got.at[pl.ds(0, 63)], got.at[pl.ds(0, 63)], rs_send).wait()
    pltpu.make_async_copy(fitted.at[pl.ds(0, 63)], fitted.at[pl.ds(0, 63)], ag_send).wait()
    for extra, many in ((True, 15), (False, 16)):
        @pl.when(has_extra == extra)
        def _():
            pltpu.make_async_copy(
                got.at[pl.ds(0, many)], got.at[pl.ds(0, many)], rs_send
            ).wait()

    @pl.when(has_extra)
    def _():
        pltpu.make_async_copy(fitted.at[pl.ds(0, 63)], fitted.at[pl.ds(0, 63)], ag_send).wait()

    @pl.when(c == owner)
    def _():
        for many in (32, 31):
            pltpu.make_async_copy(
                pieces.at[pl.ds(0, many)], pieces.at[pl.ds(0, many)], d_send
            ).wait()


def body(densities, tensor, metric, row_count):
    anywhere = pl.BlockSpec(memory_space=pl.ANY)
    dma = pltpu.SemaphoreType.DMA
    bf16, f32 = jnp.bfloat16, jnp.float32
    return pl.pallas_call(
        kernel,
        name="coulomb",
        out_shape=jax.ShapeDtypeStruct((K // 2, ROWS), bf16),
        in_specs=[pl.BlockSpec(memory_space=pltpu.SMEM), anywhere, anywhere, anywhere],
        out_specs=pl.BlockSpec(memory_space=pltpu.VMEM),
        scratch_shapes=[
            pltpu.VMEM((ROWS, AUX), bf16),
            pltpu.VMEM((COLS, AUX), bf16),
            pltpu.VMEM((K, ROWS), bf16),
            pltpu.VMEM((80, K, TILE), bf16),
            pltpu.VMEM((64, K, TILE), bf16),
            pltpu.VMEM((64, K, TILE), bf16),
            pltpu.VMEM((80, K, TILE), bf16),
            pltpu.VMEM((2, K, COLS), f32),
            pltpu.VMEM((K, COLS), bf16),
            pltpu.VMEM((32, 3, K, TILE), bf16),
            pltpu.VMEM((2, K // 2, ROWS), f32),
            pltpu.VMEM((K // 2, ROWS), f32),
            dma, dma((len(CHUNKS),)), dma, dma, dma, dma,
            dma, dma((4,)), dma((4,)), dma, dma, dma, dma((4,)), dma, dma,
        ],
        compiler_params=pltpu.CompilerParams(
            collective_id=0, has_side_effects=True, vmem_limit_bytes=56 << 20
        ),
    )(row_count, densities, tensor, metric.T)


def solution(mesh):
    placed = (P(None, "pairs"), P("pairs", "aux"), P("aux", "pairs"), P("pairs"))
    return jax.shard_map(
        body, mesh=mesh, in_specs=placed, out_specs=P("aux", "pairs"), check_vma=False
    )
```

```python
import jax
import jax.numpy as jnp
from jax import lax
from jax.experimental import pallas as pl
from jax.experimental.pallas import tpu as pltpu
from jax.sharding import PartitionSpec as P

MESH = pl.DeviceIdType.MESH
K, ROWS, AUX, COLS = 16, 768, 10240, 320
TILE, WIDTH, PLANE = 128, 1024, 2048
FLYING = 6
GATE = 2
TURN = 512
EARLY = 12


def nth(a):
    return (2 + 3 * a + 3 * (a * (a - 1) // 2)) % 4


def total_of(terms):
    while len(terms) > 1:
        terms = [sum(terms[i + 1 : i + 2], terms[i]) for i in range(0, len(terms), 2)]
    return terms[0]


def repeat(count, what):
    def one(i, carry):
        what(i)
        return carry

    lax.fori_loop(0, count, one, 0)


def kernel(
    count_hbm, dens_hbm, tensor_hbm, metric_hbm, out_ref,
    count, tv, mv, tt, mt, dv, fit, got, stage, fitted, part, piece, pieces, back, returned,
    load_n, load_d, load_t, load_m, rs_send, rs_recv,
    ag_send, ag_recv, c_send, c_recv, d_send, d_recv, e_send, e_recv,
):
    p, c = lax.axis_index("pairs"), lax.axis_index("aux")
    y, x, z = p // 16, (p // 4) % 4, p % 4
    diagonal = (x + y + z) % 4
    has_extra = diagonal == 0
    owner = p // 32
    mine = p - 32 * owner

    def chip(dy, dx, dz):
        return ((y + dy) % 4 * 4 + (x + dx) % 4) * 4 + (z + dz) % 4

    def to_all(order, act):
        def row(i):
            first, second = nth(i // 4), nth(i % 4)
            for dz in (2, 1, 3):
                act(*order(first, second), dz)

            @pl.when(i != 15)
            def _():
                act(*order(first, second), 0)

        repeat(16, row)

    load_dens = pltpu.make_async_copy(dens_hbm, dv, load_d)
    load_dens.start()
    load_count = pltpu.make_async_copy(count_hbm, count, load_n)
    load_count.start()

    def plane_of(n):
        return (y + nth(n - 1)) % 4

    def columns_of(m):
        n = m // 2
        is_main = (n + 4) // 5
        first = is_main * plane_of(n) * PLANE + (1 - is_main) * 64 * TILE + (m % 2) * WIDTH
        return pl.ds(pl.multiple_of(first, WIDTH), WIDTH)

    def load(m):
        columns = columns_of(m)
        return pltpu.make_async_copy(tensor_hbm.at[:, columns], tv.at[:, columns], load_t.at[m])

    repeat(FLYING, lambda m: load(m).start())
    load_metric = pltpu.make_async_copy(metric_hbm, mv, load_m)

    barrier = pltpu.get_barrier_semaphore()
    to_all(
        lambda a, b: (a, b),
        lambda dy, dx, dz: pl.semaphore_signal(
            barrier, inc=1, device_id=(chip(dy, dx, dz), c), device_id_type=MESH
        ),
    )
    pl.semaphore_signal(barrier, inc=1, device_id=(p, 1 - c), device_id_type=MESH)

    load_count.wait()
    load_dens.wait()
    live = lax.broadcasted_iota(jnp.int32, (K, ROWS), 1) < count[0]
    dv[...] = jnp.where(live, dv[...], jnp.zeros((K, ROWS), jnp.bfloat16))

    def send_plane(n, carry):
        dy = nth(n - 1)

        def row(i):
            dx = nth(i)
            for dz in (2, 1, 3, 0):
                q = chip(dy, dx, dz)
                elsewhere = True if dz else (n != 4) | (i != 3)
                extra = (diagonal + dy + dx + dz) % 4 == 0
                for many in (2, 1):
                    @pl.when((extra == (many == 2)) & elsewhere)
                    def _():
                        pltpu.make_async_remote_copy(
                            fit.at[pl.ds(2 * q, many)], got.at[pl.ds(2 * p, many)],
                            rs_send, rs_recv, device_id=(q, c), device_id_type=MESH,
                        ).start()

        repeat(4, row)
        return carry

    def fit_step(m):
        n = m // 2
        is_main = (n + 4) // 5
        load(m).wait()

        @pl.when(m + FLYING < AUX // WIDTH)
        def _():
            load(m + FLYING).start()

        @pl.when(m + FLYING == AUX // WIDTH)
        def _():
            load_metric.start()

        term = jnp.dot(dv[...], tv[:, columns_of(m)], preferred_element_type=jnp.float32)
        term = term.astype(jnp.bfloat16)
        for j in range(WIDTH // TILE):
            tile = (m % 2) * (WIDTH // TILE) + j
            extra = 2 * (4 * tile + (12 - tile // 4 - tile % 4) % 4) + 1
            slot = is_main * 2 * (plane_of(n) * 16 + tile) + (1 - is_main) * extra
            fit[slot] = term[:, j * TILE : (j + 1) * TILE]

        @pl.when(m == 2 * GATE + 1)
        def _():
            pl.semaphore_wait(barrier, 64)

        @pl.when((m % 2 == 1) & (n >= GATE))
        def _():
            lax.fori_loop(1 + (n - GATE + 3) // 4 * (n - 1), n + 1, send_plane, 0)

    repeat(AUX // WIDTH, fit_step)
    def turn(source, target):
        def one(i, carry):
            columns = pl.ds(pl.multiple_of(i * TURN, TURN), TURN)
            target[columns, :] = source[:, columns].T
            return carry

        return one

    for many in (2, 1):
        @pl.when(has_extra == (many == 2))
        def _():
            own = pl.ds(2 * p, many)
            pltpu.make_async_copy(fit.at[own], got.at[own], rs_recv).start()

    if EARLY:
        lax.fori_loop(0, EARLY, turn(tv, tt), 0)
    for many in (2, 1):
        @pl.when(has_extra == (many == 2))
        def _():
            everything = got.at[pl.ds(0, 64 * many)]
            pltpu.make_async_copy(everything, everything, rs_recv).wait()
            for i in range(many):
                total = total_of([got[2 * q + i].astype(jnp.float32) for q in range(64)])
                stage[i] = total.astype(jnp.bfloat16)
            share, place = stage.at[pl.ds(0, many)], fitted.at[pl.ds(2 * p, many)]
            to_all(
                lambda a, b: (a, b),
                lambda dy, dx, dz: pltpu.make_async_remote_copy(
                    share, place, ag_send, ag_recv.at[(4 - dy) % 4],
                    device_id=(chip(dy, dx, dz), c), device_id_type=MESH,
                ).start(),
            )
            pltpu.make_async_copy(share, place, ag_recv.at[0]).start()

    load_metric.wait()
    lax.fori_loop(0, AUX // TURN, turn(mv, mt), 0)
    lax.fori_loop(EARLY, AUX // TURN, turn(tv, tt), 0)

    def solve(a, half):
        dy = nth(a)
        plane = (y + dy) % 4
        arrived = fitted.at[pl.ds(0, 20)]
        pltpu.make_async_copy(arrived, arrived, ag_recv.at[dy]).wait()
        slots = [2 * (plane * 16 + i) for i in range(16)]
        extras = [2 * (plane * 16 + 4 * j + (12 - plane - j) % 4) + 1 for j in range(4)]
        for first, here in ((plane * 16, slots), (64 + plane * 4, extras)):
            rows = pl.ds(pl.multiple_of(first * TILE, 4 * TILE), len(here) * TILE)
            half += jnp.dot(
                jnp.concatenate([fitted[slot] for slot in here], axis=1), mt[rows, :],
                preferred_element_type=jnp.float32,
            )
        return half

    part[0] = lax.fori_loop(0, 4, solve, jnp.zeros((K, COLS), jnp.float32))

    exchange = pltpu.make_async_remote_copy(
        part.at[0], part.at[1], c_send, c_recv, device_id=(p, 1 - c), device_id_type=MESH
    )

    @pl.when(c != owner)
    def _():
        exchange.start()
        exchange.wait_send()

    @pl.when(c == owner)
    def _():
        exchange.wait_recv()
        whole = (part[0] + part[1]).astype(jnp.bfloat16)
        blank = jnp.zeros((K, TILE // 2), jnp.bfloat16)
        low = jnp.concatenate([whole, blank], axis=1)
        high = jnp.concatenate([blank, whole], axis=1)
        placed = jnp.where(jnp.full(low.shape, p % 2, jnp.int32) == 0, low, high)
        for i in range(3):
            piece[i] = placed[:, i * TILE : (i + 1) * TILE]
        to_all(
            lambda a, b: (b, a),
            lambda dy, dx, dz: pltpu.make_async_remote_copy(
                piece, pieces.at[mine], d_send, d_recv.at[(4 - dx) % 4],
                device_id=(chip(dy, dx, dz), c), device_id_type=MESH,
            ).start(),
        )
        pltpu.make_async_copy(piece, pieces.at[mine], d_recv.at[0]).start()

    def back_step(i, total):
        dx = nth(i // 2)
        first = i % 2 * 16 + (x + dx) % 4 * 4

        @pl.when(i % 2 == 0)
        def _():
            arrived = pieces.at[pl.ds(0, 8)]
            pltpu.make_async_copy(arrived, arrived, d_recv.at[dx]).wait()

        row = []
        for j in (0, 2):
            row += [
                pieces[first + j, 0],
                pieces[first + j, 1],
                pieces[first + j, 2] + pieces[first + j + 1, 0],
                pieces[first + j + 1, 1],
                pieces[first + j + 1, 2],
            ]
        rows = pl.ds(pl.multiple_of(first * COLS, 4 * COLS), 4 * COLS)
        return total + jnp.dot(
            jnp.concatenate(row, axis=1), tt[rows, :], preferred_element_type=jnp.float32
        )

    total = lax.fori_loop(0, 8, back_step, jnp.zeros((K, ROWS), jnp.float32))
    back[0] = total[0:8]
    back[1] = total[8:16]
    result = back[c]

    swap = pltpu.make_async_remote_copy(
        back.at[1 - c], returned, e_send, e_recv, device_id=(p, 1 - c), device_id_type=MESH
    )
    swap.start()
    swap.wait_recv()
    result = back[c] + returned[...]
    swap.wait_send()
    alive = lax.broadcasted_iota(jnp.int32, (K // 2, ROWS), 1) < count[0]
    out_ref[...] = jnp.where(alive, result, jnp.zeros_like(result))

    for extra in (True, False):
        @pl.when(has_extra == extra)
        def _():
            sent = fit.at[pl.ds(0, 78 if extra else 79)]
            pltpu.make_async_copy(sent, sent, rs_send).wait()
            sent = fitted.at[pl.ds(0, 126 if extra else 63)]
            pltpu.make_async_copy(sent, sent, ag_send).wait()

    @pl.when(c == owner)
    def _():
        for many in (32, 31):
            sent = pieces.at[pl.ds(0, many)]
            pltpu.make_async_copy(sent, sent, d_send).wait()


def body(densities, tensor, metric, row_count):
    hbm = pl.BlockSpec(memory_space=pltpu.HBM)
    dma = pltpu.SemaphoreType.DMA
    bf16, f32 = jnp.bfloat16, jnp.float32
    out = pl.pallas_call(
        kernel,
        name="coulomb",
        out_shape=pltpu.VMEM((K // 2, ROWS), f32),
        in_specs=[hbm, hbm, hbm, hbm],
        out_specs=pl.BlockSpec(memory_space=pltpu.VMEM),
        scratch_shapes=[
            pltpu.SMEM((1,), jnp.int32),
            pltpu.VMEM((ROWS, AUX), bf16),
            pltpu.VMEM((COLS, AUX), bf16),
            pltpu.VMEM((AUX, ROWS), bf16),
            pltpu.VMEM((AUX, COLS), bf16),
            pltpu.VMEM((K, ROWS), bf16),
            pltpu.VMEM((128, K, TILE), bf16),
            pltpu.VMEM((128, K, TILE), bf16),
            pltpu.VMEM((2, K, TILE), bf16),
            pltpu.VMEM((128, K, TILE), bf16),
            pltpu.VMEM((2, K, COLS), f32),
            pltpu.VMEM((3, K, TILE), bf16),
            pltpu.VMEM((32, 3, K, TILE), bf16),
            pltpu.VMEM((2, K // 2, ROWS), f32),
            pltpu.VMEM((K // 2, ROWS), f32),
            dma, dma, dma((AUX // WIDTH,)), dma, dma, dma,
            dma, dma((4,)), dma, dma, dma, dma((4,)), dma, dma,
        ],
        compiler_params=pltpu.CompilerParams(
            collective_id=0, has_side_effects=True, vmem_limit_bytes=54 << 20
        ),
    )(row_count, densities, tensor, metric.T)
    return out.astype(bf16)


def solution(mesh):
    placed = (P(None, "pairs"), P("pairs", "aux"), P("aux", "pairs"), P("pairs"))
    return jax.shard_map(
        body, mesh=mesh, in_specs=placed, out_specs=P("aux", "pairs"), check_vma=False
    )
```

```python
import jax
import jax.numpy as jnp
from jax import lax
from jax.experimental import pallas as pl
from jax.experimental.pallas import tpu as pltpu
from jax.sharding import PartitionSpec as P

MESH = pl.DeviceIdType.MESH
K, ROWS, AUX, COLS = 16, 768, 10240, 320
TILE, WIDTH, PLANE = 128, 1024, 2048
GATE = 2
TURN = 512
EARLY = 12
FIRST = 3
FLYING = 6


def nth(a):
    return (2 + 3 * a + 3 * (a * (a - 1) // 2)) % 4


def near(a):
    return (a + a * (a - 1) // 2) % 4


def total_of(terms):
    while len(terms) > 1:
        terms = [sum(terms[i + 1 : i + 2], terms[i]) for i in range(0, len(terms), 2)]
    return terms[0]


def repeat(count, what):
    def one(i, carry):
        what(i)
        return carry

    lax.fori_loop(0, count, one, 0)


def kernel(
    count_hbm, dens_hbm, tensor_hbm, metric_hbm, out_ref,
    count, tv, mv, tt, mt, dv, fit, got, stage, fitted, part, piece, pieces, back, returned,
    load_n, load_d, load_t, load_m, rs_send, rs_recv,
    ag_send, ag_recv, c_send, c_recv, d_send, d_recv, e_send, e_recv,
):
    p, c = lax.axis_index("pairs"), lax.axis_index("aux")
    y, x, z = p // 16, (p // 4) % 4, p % 4
    diagonal = (x + y + z) % 4
    has_extra = diagonal == 0
    owner = p // 32
    mine = p - 32 * owner

    def chip(dy, dx, dz):
        return ((y + dy) % 4 * 4 + (x + dx) % 4) * 4 + (z + dz) % 4

    def to_all(order, act, outer=nth):
        def block(i):
            first = outer(i)
            for second in (2, 1, 3, 0):
                for dz in (2, 1, 3, 0):
                    if second or dz:
                        act(*order(first, second), dz)
                    else:
                        @pl.when(first != 0)
                        def _():
                            act(*order(first, second), dz)

        repeat(4, block)

    load_dens = pltpu.make_async_copy(dens_hbm, dv, load_d)
    load_dens.start()
    load_count = pltpu.make_async_copy(count_hbm, count, load_n)
    load_count.start()

    def plane_of(n):
        return (y + nth(n - 1)) % 4

    def columns_of(m):
        n = m // 2
        is_main = (n + 4) // 5
        first = is_main * plane_of(n) * PLANE + (1 - is_main) * 64 * TILE + (m % 2) * WIDTH
        return pl.ds(pl.multiple_of(first, WIDTH), WIDTH)

    def load(m):
        columns = columns_of(m)
        return pltpu.make_async_copy(tensor_hbm.at[:, columns], tv.at[:, columns], load_t.at[m])

    repeat(FIRST, lambda m: load(m).start())
    barrier = pltpu.get_barrier_semaphore()
    to_all(
        lambda a, b: (a, b),
        lambda dy, dx, dz: pl.semaphore_signal(
            barrier, inc=1, device_id=(chip(dy, dx, dz), c), device_id_type=MESH
        ),
    )
    pl.semaphore_signal(barrier, inc=1, device_id=(p, 1 - c), device_id_type=MESH)

    lax.fori_loop(FIRST, FLYING, lambda m, carry: (load(m).start(), carry)[1], 0)
    load_metric = pltpu.make_async_copy(metric_hbm, mv, load_m)

    load_count.wait()
    load_dens.wait()
    live = lax.broadcasted_iota(jnp.int32, (K, ROWS), 1) < count[0]
    dv[...] = jnp.where(live, dv[...], jnp.zeros((K, ROWS), jnp.bfloat16))

    def send_fit(dy, dx, dz, many):
        q = chip(dy, dx, dz)
        pltpu.make_async_remote_copy(
            fit.at[pl.ds(2 * q, many)], got.at[pl.ds(2 * p, many)],
            rs_send, rs_recv, device_id=(q, c), device_id_type=MESH,
        ).start()

    def send_plane(n, carry):
        dy = nth(n - 1)
        lead = 16 - diagonal - dy

        def row(dx):
            for dz, many in ((0, 2), (2, 1), (1, 1), (3, 1)):
                send_fit(dy, dx, lead - dx + dz, many)

        for dx in (2, 1, 3):
            row(dx)
        @pl.when(dy != 0)
        def _():
            row(0)

        @pl.when(dy == 0)
        def _():
            for dz in (2, 1, 3):
                for many in (2, 1):
                    @pl.when(((diagonal + dz) % 4 == 0) == (many == 2))
                    def _():
                        send_fit(0, 0, dz, many)

        return carry

    def fit_step(m):
        n = m // 2
        is_main = (n + 4) // 5
        load(m).wait()

        @pl.when(m + FLYING < AUX // WIDTH)
        def _():
            load(m + FLYING).start()

        term = jnp.dot(dv[...], tv[:, columns_of(m)], preferred_element_type=jnp.float32)
        term = term.astype(jnp.bfloat16)
        for j in range(WIDTH // TILE):
            tile = (m % 2) * (WIDTH // TILE) + j
            extra = 2 * (4 * tile + (12 - tile // 4 - tile % 4) % 4) + 1
            slot = is_main * 2 * (plane_of(n) * 16 + tile) + (1 - is_main) * extra
            fit[slot] = term[:, j * TILE : (j + 1) * TILE]

        @pl.when(m == 2 * GATE + 1)
        def _():
            pl.semaphore_wait(barrier, 64)

        @pl.when((m % 2 == 1) & (n >= GATE))
        def _():
            lax.fori_loop(1 + (n - GATE + 3) // 4 * (n - 1), n + 1, send_plane, 0)

    repeat(AUX // WIDTH, fit_step)
    load_metric.start()
    def turn(source, target):
        def one(i, carry):
            columns = pl.ds(pl.multiple_of(i * TURN, TURN), TURN)
            target[columns, :] = source[:, columns].T
            return carry

        return one

    for many in (2, 1):
        @pl.when(has_extra == (many == 2))
        def _():
            own = pl.ds(2 * p, many)
            pltpu.make_async_copy(fit.at[own], got.at[own], rs_recv).start()

    lax.fori_loop(0, EARLY, turn(tv, tt), 0)
    for many in (2, 1):
        @pl.when(has_extra == (many == 2))
        def _():
            everything = got.at[pl.ds(0, 64 * many)]
            pltpu.make_async_copy(everything, everything, rs_recv).wait()
            for i in range(many):
                total = total_of([got[2 * q + i].astype(jnp.float32) for q in range(64)])
                stage[i] = total.astype(jnp.bfloat16)
            share, place = stage.at[pl.ds(0, many)], fitted.at[pl.ds(2 * p, many)]
            to_all(
                lambda a, b: (a, b),
                lambda dy, dx, dz: pltpu.make_async_remote_copy(
                    share, place, ag_send, ag_recv.at[(4 - dy) % 4],
                    device_id=(chip(dy, dx, dz), c), device_id_type=MESH,
                ).start(), nth,
            )
            pltpu.make_async_copy(share, place, ag_recv.at[0]).start()

    load_metric.wait()
    lax.fori_loop(0, AUX // TURN, turn(mv, mt), 0)
    lax.fori_loop(EARLY, AUX // TURN, turn(tv, tt), 0)

    def solve(a, half):
        dy = nth(a)
        plane = (y + dy) % 4
        arrived = fitted.at[pl.ds(0, 20)]
        pltpu.make_async_copy(arrived, arrived, ag_recv.at[dy]).wait()
        slots = [2 * (plane * 16 + i) for i in range(16)]
        extras = [2 * (plane * 16 + 4 * j + (12 - plane - j) % 4) + 1 for j in range(4)]
        for first, here in ((plane * 16, slots), (64 + plane * 4, extras)):
            rows = pl.ds(pl.multiple_of(first * TILE, 4 * TILE), len(here) * TILE)
            half += jnp.dot(
                jnp.concatenate([fitted[slot] for slot in here], axis=1), mt[rows, :],
                preferred_element_type=jnp.float32,
            )
        return half

    part[0] = lax.fori_loop(0, 4, solve, jnp.zeros((K, COLS), jnp.float32))

    exchange = pltpu.make_async_remote_copy(
        part.at[0], part.at[1], c_send, c_recv, device_id=(p, 1 - c), device_id_type=MESH
    )

    @pl.when(c != owner)
    def _():
        exchange.start()
        exchange.wait_send()

    @pl.when(c == owner)
    def _():
        exchange.wait_recv()
        whole = part[0] + part[1]
        even = jnp.full((K, 2 * TILE), p % 2, jnp.int32) == 0
        full = jnp.where(even, whole[:, 0 : 2 * TILE], whole[:, TILE // 2 : COLS])
        rest = jnp.where(
            even[:, 0 : TILE // 2], whole[:, 2 * TILE : COLS], whole[:, 0 : TILE // 2]
        )
        both = jnp.concatenate([rest[0:8], rest[8:16]], axis=1)
        for i, half_tile in enumerate((
            full[0:8, 0:TILE], full[8:16, 0:TILE],
            full[0:8, TILE:], full[8:16, TILE:], both,
        )):
            piece[i] = half_tile.astype(jnp.bfloat16)
        to_all(
            lambda a, b: (b, a),
            lambda dy, dx, dz: pltpu.make_async_remote_copy(
                piece, pieces.at[mine], d_send, d_recv.at[(4 - dx) % 4],
                device_id=(chip(dy, dx, dz), c), device_id_type=MESH,
            ).start(), near,
        )
        pltpu.make_async_copy(piece, pieces.at[mine], d_recv.at[0]).start()

    def back_step(i, total):
        dx = near(i // 2)
        first = i % 2 * 16 + (x + dx) % 4 * 4

        @pl.when(i % 2 == 0)
        def _():
            arrived = pieces.at[pl.ds(0, 8)]
            pltpu.make_async_copy(arrived, arrived, d_recv.at[dx]).wait()

        upper, lower = [], []
        for j in (0, 2):
            left, right = pieces[first + j, 4], pieces[first + j + 1, 4]
            middle = TILE // 2
            upper += [
                pieces[first + j, 0], pieces[first + j, 2],
                jnp.concatenate([left[:, :middle], right[:, :middle]], axis=1),
                pieces[first + j + 1, 0], pieces[first + j + 1, 2],
            ]
            lower += [
                pieces[first + j, 1], pieces[first + j, 3],
                jnp.concatenate([left[:, middle:], right[:, middle:]], axis=1),
                pieces[first + j + 1, 1], pieces[first + j + 1, 3],
            ]
        row = [jnp.concatenate(pair, axis=0) for pair in zip(upper, lower)]
        rows = pl.ds(pl.multiple_of(first * COLS, 4 * COLS), 4 * COLS)
        return total + jnp.dot(
            jnp.concatenate(row, axis=1), tt[rows, :], preferred_element_type=jnp.float32
        )

    total = lax.fori_loop(0, 8, back_step, jnp.zeros((K, ROWS), jnp.float32))
    back[0] = total[0:8]
    back[1] = total[8:16]
    result = back[c]

    swap = pltpu.make_async_remote_copy(
        back.at[1 - c], returned, e_send, e_recv, device_id=(p, 1 - c), device_id_type=MESH
    )
    swap.start()
    swap.wait_recv()
    result = back[c] + returned[...]
    swap.wait_send()
    alive = lax.broadcasted_iota(jnp.int32, (K // 2, ROWS), 1) < count[0]
    out_ref[...] = jnp.where(alive, result, jnp.zeros_like(result))

    for extra in (True, False):
        @pl.when(has_extra == extra)
        def _():
            sent = fit.at[pl.ds(0, 78 if extra else 79)]
            pltpu.make_async_copy(sent, sent, rs_send).wait()
            sent = fitted.at[pl.ds(0, 126 if extra else 63)]
            pltpu.make_async_copy(sent, sent, ag_send).wait()

    @pl.when(c == owner)
    def _():
        for many in (32, 31):
            sent = pieces.at[pl.ds(0, many)]
            pltpu.make_async_copy(sent, sent, d_send).wait()


def body(densities, tensor, metric, row_count):
    hbm = pl.BlockSpec(memory_space=pltpu.HBM)
    dma = pltpu.SemaphoreType.DMA
    bf16, f32 = jnp.bfloat16, jnp.float32
    out = pl.pallas_call(
        kernel,
        name="coulomb",
        out_shape=pltpu.VMEM((K // 2, ROWS), f32),
        in_specs=[hbm, hbm, hbm, hbm],
        out_specs=pl.BlockSpec(memory_space=pltpu.VMEM),
        scratch_shapes=[
            pltpu.SMEM((1,), jnp.int32),
            pltpu.VMEM((ROWS, AUX), bf16),
            pltpu.VMEM((COLS, AUX), bf16),
            pltpu.VMEM((AUX, ROWS), bf16),
            pltpu.VMEM((AUX, COLS), bf16),
            pltpu.VMEM((K, ROWS), bf16),
            pltpu.VMEM((128, K, TILE), bf16),
            pltpu.VMEM((128, K, TILE), bf16),
            pltpu.VMEM((2, K, TILE), bf16),
            pltpu.VMEM((128, K, TILE), bf16),
            pltpu.VMEM((2, K, COLS), f32),
            pltpu.VMEM((5, 8, TILE), bf16),
            pltpu.VMEM((32, 5, 8, TILE), bf16),
            pltpu.VMEM((2, K // 2, ROWS), f32),
            pltpu.VMEM((K // 2, ROWS), f32),
            dma, dma, dma((AUX // WIDTH,)), dma, dma, dma,
            dma, dma((4,)), dma, dma, dma, dma((4,)), dma, dma,
        ],
        compiler_params=pltpu.CompilerParams(
            collective_id=0, has_side_effects=True, vmem_limit_bytes=54 << 20
        ),
    )(row_count, densities, tensor, metric.T)
    return out.astype(bf16)


def solution(mesh):
    placed = (P(None, "pairs"), P("pairs", "aux"), P("aux", "pairs"), P("pairs"))
    return jax.shard_map(
        body, mesh=mesh, in_specs=placed, out_specs=P("aux", "pairs"), check_vma=False
    )
```

```python
import jax
import jax.numpy as jnp
from jax import lax
from jax.experimental import pallas as pl
from jax.experimental.pallas import tpu as pltpu
from jax.sharding import PartitionSpec as P

MESH = pl.DeviceIdType.MESH
K, ROWS, AUX, COLS = 16, 768, 10240, 320
TILE, WIDTH, PLANE = 128, 1024, 2048
GATE = 2
TURN = 512
EARLY = 12
FIRST = 3
FLYING = 6


def nth(a):
    return (2 + 3 * a + 3 * (a * (a - 1) // 2)) % 4


def near(a):
    return (a + a * (a - 1) // 2) % 4


def total_of(terms):
    while len(terms) > 1:
        terms = [sum(terms[i + 1 : i + 2], terms[i]) for i in range(0, len(terms), 2)]
    return terms[0]


def repeat(count, what):
    def one(i, carry):
        what(i)
        return carry

    lax.fori_loop(0, count, one, 0)


def kernel(
    count_hbm, dens_hbm, tensor_hbm, metric_hbm, out_ref,
    count, tv, mv, tt, mt, dv, fit, got, stage, fitted, part, piece, pieces, back, returned,
    load_n, load_d, load_t, load_m, rs_send, rs_recv,
    ag_send, ag_recv, c_send, c_recv, d_send, d_recv, e_send, e_recv,
):
    p, c = lax.axis_index("pairs"), lax.axis_index("aux")
    y, x, z = p // 16, (p // 4) % 4, p % 4
    diagonal = (x + y + z + 2 * c) % 4
    has_extra = diagonal == 0
    owner = p // 32
    mine = p - 32 * owner

    def chip(dy, dx, dz):
        return ((y + dy) % 4 * 4 + (x + dx) % 4) * 4 + (z + dz) % 4

    def to_all(order, act, outer=nth):
        def block(i):
            first = outer(i)
            for second in (2, 1, 3, 0):
                for dz in (2, 1, 3, 0):
                    if second or dz:
                        act(*order(first, second), dz)
                    else:
                        @pl.when(first != 0)
                        def _():
                            act(*order(first, second), dz)

        repeat(4, block)

    load_dens = pltpu.make_async_copy(dens_hbm, dv, load_d)
    load_dens.start()
    load_count = pltpu.make_async_copy(count_hbm, count, load_n)
    load_count.start()

    def plane_of(n):
        return (y + nth(n - 1)) % 4

    def columns_of(m):
        n = m // 2
        is_main = (n + 4) // 5
        first = is_main * plane_of(n) * PLANE + (1 - is_main) * 64 * TILE + (m % 2) * WIDTH
        return pl.ds(pl.multiple_of(first, WIDTH), WIDTH)

    def load(m):
        columns = columns_of(m)
        return pltpu.make_async_copy(tensor_hbm.at[:, columns], tv.at[:, columns], load_t.at[m])

    repeat(FIRST, lambda m: load(m).start())
    barrier = pltpu.get_barrier_semaphore()
    to_all(
        lambda a, b: (a, b),
        lambda dy, dx, dz: pl.semaphore_signal(
            barrier, inc=1, device_id=(chip(dy, dx, dz), c), device_id_type=MESH
        ),
    )
    pl.semaphore_signal(barrier, inc=1, device_id=(p, 1 - c), device_id_type=MESH)

    lax.fori_loop(FIRST, FLYING, lambda m, carry: (load(m).start(), carry)[1], 0)
    load_metric = pltpu.make_async_copy(metric_hbm, mv, load_m)

    load_count.wait()
    load_dens.wait()
    live = lax.broadcasted_iota(jnp.int32, (K, ROWS), 1) < count[0]
    dv[...] = jnp.where(live, dv[...], jnp.zeros((K, ROWS), jnp.bfloat16))

    def send_fit(dy, dx, dz, many):
        q = chip(dy, dx, dz)
        pltpu.make_async_remote_copy(
            fit.at[pl.ds(2 * q, many)], got.at[pl.ds(2 * p, many)],
            rs_send, rs_recv, device_id=(q, c), device_id_type=MESH,
        ).start()

    def send_plane(n, carry):
        dy = nth(n - 1)
        lead = 16 - diagonal - dy

        def row(dx):
            for dz, many in ((0, 2), (2, 1), (1, 1), (3, 1)):
                send_fit(dy, dx, lead - dx + dz, many)

        for dx in (2, 1, 3):
            row(dx)
        @pl.when(dy != 0)
        def _():
            row(0)

        @pl.when(dy == 0)
        def _():
            for dz in (2, 1, 3):
                for many in (2, 1):
                    @pl.when(((diagonal + dz) % 4 == 0) == (many == 2))
                    def _():
                        send_fit(0, 0, dz, many)

        return carry

    def fit_step(m):
        n = m // 2
        is_main = (n + 4) // 5
        load(m).wait()

        @pl.when(m + FLYING < AUX // WIDTH)
        def _():
            load(m + FLYING).start()

        term = jnp.dot(dv[...], tv[:, columns_of(m)], preferred_element_type=jnp.float32)
        term = term.astype(jnp.bfloat16)
        for j in range(WIDTH // TILE):
            tile = (m % 2) * (WIDTH // TILE) + j
            extra = 2 * (4 * tile + (12 - tile // 4 - tile % 4 - 2 * c) % 4) + 1
            slot = is_main * 2 * (plane_of(n) * 16 + tile) + (1 - is_main) * extra
            fit[slot] = term[:, j * TILE : (j + 1) * TILE]

        @pl.when(m == 2 * GATE + 1)
        def _():
            pl.semaphore_wait(barrier, 64)

        @pl.when((m % 2 == 1) & (n >= GATE))
        def _():
            lax.fori_loop(1 + (n - GATE + 3) // 4 * (n - 1), n + 1, send_plane, 0)

    repeat(AUX // WIDTH, fit_step)
    load_metric.start()
    def turn(source, target):
        def one(i, carry):
            columns = pl.ds(pl.multiple_of(i * TURN, TURN), TURN)
            target[columns, :] = source[:, columns].T
            return carry

        return one

    for many in (2, 1):
        @pl.when(has_extra == (many == 2))
        def _():
            own = pl.ds(2 * p, many)
            pltpu.make_async_copy(fit.at[own], got.at[own], rs_recv).start()

    lax.fori_loop(0, EARLY, turn(tv, tt), 0)
    for many in (2, 1):
        @pl.when(has_extra == (many == 2))
        def _():
            everything = got.at[pl.ds(0, 64 * many)]
            pltpu.make_async_copy(everything, everything, rs_recv).wait()
            for i in range(many):
                total = total_of([got[2 * q + i].astype(jnp.float32) for q in range(64)])
                stage[i] = total.astype(jnp.bfloat16)
            share, place = stage.at[pl.ds(0, many)], fitted.at[pl.ds(2 * p, many)]
            to_all(
                lambda a, b: (a, b),
                lambda dy, dx, dz: pltpu.make_async_remote_copy(
                    share, place, ag_send, ag_recv.at[(4 - dy) % 4],
                    device_id=(chip(dy, dx, dz), c), device_id_type=MESH,
                ).start(), nth,
            )
            pltpu.make_async_copy(share, place, ag_recv.at[0]).start()

    load_metric.wait()
    lax.fori_loop(0, AUX // TURN, turn(mv, mt), 0)
    lax.fori_loop(EARLY, AUX // TURN, turn(tv, tt), 0)

    def solve(a, half):
        dy = nth(a)
        plane = (y + dy) % 4
        arrived = fitted.at[pl.ds(0, 20)]
        pltpu.make_async_copy(arrived, arrived, ag_recv.at[dy]).wait()
        slots = [2 * (plane * 16 + i) for i in range(16)]
        extras = [2 * (plane * 16 + 4 * j + (12 - plane - j - 2 * c) % 4) + 1 for j in range(4)]
        for first, here in ((plane * 16, slots), (64 + plane * 4, extras)):
            rows = pl.ds(pl.multiple_of(first * TILE, 4 * TILE), len(here) * TILE)
            half += jnp.dot(
                jnp.concatenate([fitted[slot] for slot in here], axis=1), mt[rows, :],
                preferred_element_type=jnp.float32,
            )
        return half

    part[0] = lax.fori_loop(0, 4, solve, jnp.zeros((K, COLS), jnp.float32))

    exchange = pltpu.make_async_remote_copy(
        part.at[0], part.at[1], c_send, c_recv, device_id=(p, 1 - c), device_id_type=MESH
    )

    @pl.when(c != owner)
    def _():
        exchange.start()
        exchange.wait_send()

    @pl.when(c == owner)
    def _():
        exchange.wait_recv()
        whole = part[0] + part[1]
        even = jnp.full((K, 2 * TILE), p % 2, jnp.int32) == 0
        full = jnp.where(even, whole[:, 0 : 2 * TILE], whole[:, TILE // 2 : COLS])
        rest = jnp.where(
            even[:, 0 : TILE // 2], whole[:, 2 * TILE : COLS], whole[:, 0 : TILE // 2]
        )
        both = jnp.concatenate([rest[0:8], rest[8:16]], axis=1)
        for i, half_tile in enumerate((
            full[0:8, 0:TILE], full[8:16, 0:TILE],
            full[0:8, TILE:], full[8:16, TILE:], both,
        )):
            piece[i] = half_tile.astype(jnp.bfloat16)
        to_all(
            lambda a, b: (b, a),
            lambda dy, dx, dz: pltpu.make_async_remote_copy(
                piece, pieces.at[mine], d_send, d_recv.at[(4 - dx) % 4],
                device_id=(chip(dy, dx, dz), c), device_id_type=MESH,
            ).start(), near,
        )
        pltpu.make_async_copy(piece, pieces.at[mine], d_recv.at[0]).start()

    def back_step(i, total):
        dx = near(i // 2)
        first = i % 2 * 16 + (x + dx) % 4 * 4

        @pl.when(i % 2 == 0)
        def _():
            arrived = pieces.at[pl.ds(0, 8)]
            pltpu.make_async_copy(arrived, arrived, d_recv.at[dx]).wait()

        upper, lower = [], []
        for j in (0, 2):
            left, right = pieces[first + j, 4], pieces[first + j + 1, 4]
            middle = TILE // 2
            upper += [
                pieces[first + j, 0], pieces[first + j, 2],
                jnp.concatenate([left[:, :middle], right[:, :middle]], axis=1),
                pieces[first + j + 1, 0], pieces[first + j + 1, 2],
            ]
            lower += [
                pieces[first + j, 1], pieces[first + j, 3],
                jnp.concatenate([left[:, middle:], right[:, middle:]], axis=1),
                pieces[first + j + 1, 1], pieces[first + j + 1, 3],
            ]
        row = [jnp.concatenate(pair, axis=0) for pair in zip(upper, lower)]
        rows = pl.ds(pl.multiple_of(first * COLS, 4 * COLS), 4 * COLS)
        return total + jnp.dot(
            jnp.concatenate(row, axis=1), tt[rows, :], preferred_element_type=jnp.float32
        )

    total = lax.fori_loop(0, 8, back_step, jnp.zeros((K, ROWS), jnp.float32))
    back[0] = total[0:8]
    back[1] = total[8:16]
    result = back[c]

    swap = pltpu.make_async_remote_copy(
        back.at[1 - c], returned, e_send, e_recv, device_id=(p, 1 - c), device_id_type=MESH
    )
    swap.start()
    swap.wait_recv()
    result = back[c] + returned[...]
    swap.wait_send()
    alive = lax.broadcasted_iota(jnp.int32, (K // 2, ROWS), 1) < count[0]
    out_ref[...] = jnp.where(alive, result, jnp.zeros_like(result))

    for extra in (True, False):
        @pl.when(has_extra == extra)
        def _():
            sent = fit.at[pl.ds(0, 78 if extra else 79)]
            pltpu.make_async_copy(sent, sent, rs_send).wait()
            sent = fitted.at[pl.ds(0, 126 if extra else 63)]
            pltpu.make_async_copy(sent, sent, ag_send).wait()

    @pl.when(c == owner)
    def _():
        for many in (32, 31):
            sent = pieces.at[pl.ds(0, many)]
            pltpu.make_async_copy(sent, sent, d_send).wait()


def body(densities, tensor, metric, row_count):
    hbm = pl.BlockSpec(memory_space=pltpu.HBM)
    dma = pltpu.SemaphoreType.DMA
    bf16, f32 = jnp.bfloat16, jnp.float32
    out = pl.pallas_call(
        kernel,
        name="coulomb",
        out_shape=pltpu.VMEM((K // 2, ROWS), f32),
        in_specs=[hbm, hbm, hbm, hbm],
        out_specs=pl.BlockSpec(memory_space=pltpu.VMEM),
        scratch_shapes=[
            pltpu.SMEM((1,), jnp.int32),
            pltpu.VMEM((ROWS, AUX), bf16),
            pltpu.VMEM((COLS, AUX), bf16),
            pltpu.VMEM((AUX, ROWS), bf16),
            pltpu.VMEM((AUX, COLS), bf16),
            pltpu.VMEM((K, ROWS), bf16),
            pltpu.VMEM((128, K, TILE), bf16),
            pltpu.VMEM((128, K, TILE), bf16),
            pltpu.VMEM((2, K, TILE), bf16),
            pltpu.VMEM((128, K, TILE), bf16),
            pltpu.VMEM((2, K, COLS), f32),
            pltpu.VMEM((5, 8, TILE), bf16),
            pltpu.VMEM((32, 5, 8, TILE), bf16),
            pltpu.VMEM((2, K // 2, ROWS), f32),
            pltpu.VMEM((K // 2, ROWS), f32),
            dma, dma, dma((AUX // WIDTH,)), dma, dma, dma,
            dma, dma((4,)), dma, dma, dma, dma((4,)), dma, dma,
        ],
        compiler_params=pltpu.CompilerParams(
            collective_id=0, has_side_effects=True, vmem_limit_bytes=54 << 20
        ),
    )(row_count, densities, tensor, metric.T)
    return out.astype(bf16)


def solution(mesh):
    placed = (P(None, "pairs"), P("pairs", "aux"), P("aux", "pairs"), P("pairs"))
    return jax.shard_map(
        body, mesh=mesh, in_specs=placed, out_specs=P("aux", "pairs"), check_vma=False
    )
```

```python
import jax
import jax.numpy as jnp
from jax import lax
from jax.experimental import pallas as pl
from jax.experimental.pallas import tpu as pltpu
from jax.sharding import PartitionSpec as P

MESH = pl.DeviceIdType.MESH
K, ROWS, AUX, COLS = 16, 768, 10240, 320
TILE, WIDTH, PLANE = 128, 1024, 2048
GATE = 2
TURN = 512
EARLY = 12
FIRST = 3
FLYING = 6


def nth(a):
    return (2 + 3 * a + 3 * (a * (a - 1) // 2)) % 4


def near(a):
    return (a + a * (a - 1) // 2) % 4


def total_of(terms):
    while len(terms) > 1:
        terms = [sum(terms[i + 1 : i + 2], terms[i]) for i in range(0, len(terms), 2)]
    return terms[0]


def repeat(count, what):
    def one(i, carry):
        what(i)
        return carry

    lax.fori_loop(0, count, one, 0)


def kernel(
    count_hbm, dens_hbm, tensor_hbm, metric_hbm, out_ref,
    count, tv, mv, tt, mt, dv, fit, got, stage, fitted, part, piece, pieces, back, returned,
    load_n, load_d, load_t, load_m, rs_send, rs_recv,
    ag_send, ag_recv, c_send, c_recv, d_send, d_recv, e_send, e_recv,
):
    p, c = lax.axis_index("pairs"), lax.axis_index("aux")
    y, x, z = p // 16, (p // 4) % 4, p % 4
    diagonal = (x + y + z + 2 * c) % 4
    has_extra = diagonal == 0
    owner = p // 32
    mine = p - 32 * owner

    def chip(dy, dx, dz):
        return ((y + dy) % 4 * 4 + (x + dx) % 4) * 4 + (z + dz) % 4

    def to_all(order, act, outer=nth):
        def block(i):
            first = outer(i)
            for second in (2, 1, 3, 0):
                for dz in (2, 1, 3, 0):
                    if second or dz:
                        act(*order(first, second), dz)
                    else:
                        @pl.when(first != 0)
                        def _():
                            act(*order(first, second), dz)

        repeat(4, block)

    def plane_of(n):
        return (y + nth(n - 1)) % 4

    def columns_of(m):
        n = m // 2
        is_main = (n + 4) // 5
        first = is_main * plane_of(n) * PLANE + (1 - is_main) * 64 * TILE + (m % 2) * WIDTH
        return pl.ds(pl.multiple_of(first, WIDTH), WIDTH)

    def load(m):
        columns = columns_of(m)
        return pltpu.make_async_copy(tensor_hbm.at[:, columns], tv.at[:, columns], load_t.at[m])

    repeat(FIRST, lambda m: load(m).start())
    load_dens = pltpu.make_async_copy(dens_hbm, dv, load_d)
    load_dens.start()
    load_count = pltpu.make_async_copy(count_hbm, count, load_n)
    load_count.start()
    barrier = pltpu.get_barrier_semaphore()
    to_all(
        lambda a, b: (a, b),
        lambda dy, dx, dz: pl.semaphore_signal(
            barrier, inc=1, device_id=(chip(dy, dx, dz), c), device_id_type=MESH
        ),
    )
    pl.semaphore_signal(barrier, inc=1, device_id=(p, 1 - c), device_id_type=MESH)

    lax.fori_loop(FIRST, FLYING, lambda m, carry: (load(m).start(), carry)[1], 0)
    load_metric = pltpu.make_async_copy(metric_hbm, mv, load_m)

    load_count.wait()
    load_dens.wait()
    live = lax.broadcasted_iota(jnp.int32, (K, ROWS), 1) < count[0]
    dv[...] = jnp.where(live, dv[...], jnp.zeros((K, ROWS), jnp.bfloat16))

    def send_fit(dy, dx, dz, many):
        q = chip(dy, dx, dz)
        pltpu.make_async_remote_copy(
            fit.at[pl.ds(2 * q, many)], got.at[pl.ds(2 * p, many)],
            rs_send, rs_recv, device_id=(q, c), device_id_type=MESH,
        ).start()

    def send_plane(n, carry):
        dy = nth(n - 1)
        lead = 16 - diagonal - dy

        def row(dx):
            for dz, many in ((0, 2), (2, 1), (1, 1), (3, 1)):
                send_fit(dy, dx, lead - dx + dz, many)

        for dx in (2, 1, 3):
            row(dx)
        @pl.when(dy != 0)
        def _():
            row(0)

        @pl.when(dy == 0)
        def _():
            for dz in (2, 1, 3):
                for many in (2, 1):
                    @pl.when(((diagonal + dz) % 4 == 0) == (many == 2))
                    def _():
                        send_fit(0, 0, dz, many)

        return carry

    def fit_step(m):
        n = m // 2
        is_main = (n + 4) // 5
        load(m).wait()

        @pl.when(m + FLYING < AUX // WIDTH)
        def _():
            load(m + FLYING).start()

        term = jnp.dot(dv[...], tv[:, columns_of(m)], preferred_element_type=jnp.float32)
        term = term.astype(jnp.bfloat16)
        for j in range(WIDTH // TILE):
            tile = (m % 2) * (WIDTH // TILE) + j
            extra = 2 * (4 * tile + (12 - tile // 4 - tile % 4 - 2 * c) % 4) + 1
            slot = is_main * 2 * (plane_of(n) * 16 + tile) + (1 - is_main) * extra
            fit[slot] = term[:, j * TILE : (j + 1) * TILE]

        @pl.when(m == 2 * GATE + 1)
        def _():
            pl.semaphore_wait(barrier, 64)

        @pl.when((m % 2 == 1) & (n >= GATE))
        def _():
            lax.fori_loop(1 + (n - GATE + 3) // 4 * (n - 1), n + 1, send_plane, 0)

    repeat(AUX // WIDTH, fit_step)
    load_metric.start()
    def turn(source, target):
        def one(i, carry):
            columns = pl.ds(pl.multiple_of(i * TURN, TURN), TURN)
            target[columns, :] = source[:, columns].T
            return carry

        return one

    for many in (2, 1):
        @pl.when(has_extra == (many == 2))
        def _():
            own = pl.ds(2 * p, many)
            pltpu.make_async_copy(fit.at[own], got.at[own], rs_recv).start()

    lax.fori_loop(0, EARLY, turn(tv, tt), 0)
    for many in (2, 1):
        @pl.when(has_extra == (many == 2))
        def _():
            everything = got.at[pl.ds(0, 64 * many)]
            pltpu.make_async_copy(everything, everything, rs_recv).wait()
            for i in range(many):
                total = total_of([got[2 * q + i].astype(jnp.float32) for q in range(64)])
                stage[i] = total.astype(jnp.bfloat16)
            share, place = stage.at[pl.ds(0, many)], fitted.at[pl.ds(2 * p, many)]
            to_all(
                lambda a, b: (a, b),
                lambda dy, dx, dz: pltpu.make_async_remote_copy(
                    share, place, ag_send, ag_recv.at[(4 - dy) % 4],
                    device_id=(chip(dy, dx, dz), c), device_id_type=MESH,
                ).start(), nth,
            )
            pltpu.make_async_copy(share, place, ag_recv.at[0]).start()

    load_metric.wait()
    lax.fori_loop(0, AUX // TURN, turn(mv, mt), 0)
    lax.fori_loop(EARLY, AUX // TURN, turn(tv, tt), 0)

    def solve(a, half):
        dy = nth(a)
        plane = (y + dy) % 4
        arrived = fitted.at[pl.ds(0, 20)]
        pltpu.make_async_copy(arrived, arrived, ag_recv.at[dy]).wait()
        slots = [2 * (plane * 16 + i) for i in range(16)]
        extras = [2 * (plane * 16 + 4 * j + (12 - plane - j - 2 * c) % 4) + 1 for j in range(4)]
        for first, here in ((plane * 16, slots), (64 + plane * 4, extras)):
            rows = pl.ds(pl.multiple_of(first * TILE, 4 * TILE), len(here) * TILE)
            half += jnp.dot(
                jnp.concatenate([fitted[slot] for slot in here], axis=1), mt[rows, :],
                preferred_element_type=jnp.float32,
            )
        return half

    part[0] = lax.fori_loop(0, 4, solve, jnp.zeros((K, COLS), jnp.float32))

    exchange = pltpu.make_async_remote_copy(
        part.at[0], part.at[1], c_send, c_recv, device_id=(p, 1 - c), device_id_type=MESH
    )

    @pl.when(c != owner)
    def _():
        exchange.start()
        exchange.wait_send()

    @pl.when(c == owner)
    def _():
        exchange.wait_recv()
        whole = part[0] + part[1]
        even = jnp.full((K, 2 * TILE), p % 2, jnp.int32) == 0
        full = jnp.where(even, whole[:, 0 : 2 * TILE], whole[:, TILE // 2 : COLS])
        rest = jnp.where(
            even[:, 0 : TILE // 2], whole[:, 2 * TILE : COLS], whole[:, 0 : TILE // 2]
        )
        both = jnp.concatenate([rest[0:8], rest[8:16]], axis=1)
        for i, half_tile in enumerate((
            full[0:8, 0:TILE], full[8:16, 0:TILE],
            full[0:8, TILE:], full[8:16, TILE:], both,
        )):
            piece[i] = half_tile.astype(jnp.bfloat16)
        to_all(
            lambda a, b: (b, a),
            lambda dy, dx, dz: pltpu.make_async_remote_copy(
                piece, pieces.at[mine], d_send, d_recv.at[(4 - dx) % 4],
                device_id=(chip(dy, dx, dz), c), device_id_type=MESH,
            ).start(), near,
        )
        pltpu.make_async_copy(piece, pieces.at[mine], d_recv.at[0]).start()

    def back_step(i, total):
        dx = near(i // 2)
        first = i % 2 * 16 + (x + dx) % 4 * 4

        @pl.when(i % 2 == 0)
        def _():
            arrived = pieces.at[pl.ds(0, 8)]
            pltpu.make_async_copy(arrived, arrived, d_recv.at[dx]).wait()

        upper, lower = [], []
        for j in (0, 2):
            left, right = pieces[first + j, 4], pieces[first + j + 1, 4]
            middle = TILE // 2
            upper += [
                pieces[first + j, 0], pieces[first + j, 2],
                jnp.concatenate([left[:, :middle], right[:, :middle]], axis=1),
                pieces[first + j + 1, 0], pieces[first + j + 1, 2],
            ]
            lower += [
                pieces[first + j, 1], pieces[first + j, 3],
                jnp.concatenate([left[:, middle:], right[:, middle:]], axis=1),
                pieces[first + j + 1, 1], pieces[first + j + 1, 3],
            ]
        row = [jnp.concatenate(pair, axis=0) for pair in zip(upper, lower)]
        rows = pl.ds(pl.multiple_of(first * COLS, 4 * COLS), 4 * COLS)
        return total + jnp.dot(
            jnp.concatenate(row, axis=1), tt[rows, :], preferred_element_type=jnp.float32
        )

    total = lax.fori_loop(0, 8, back_step, jnp.zeros((K, ROWS), jnp.float32))
    back[0] = total[0:8]
    back[1] = total[8:16]
    result = back[c]

    swap = pltpu.make_async_remote_copy(
        back.at[1 - c], returned, e_send, e_recv, device_id=(p, 1 - c), device_id_type=MESH
    )
    swap.start()
    swap.wait_recv()
    result = back[c] + returned[...]
    swap.wait_send()
    alive = lax.broadcasted_iota(jnp.int32, (K // 2, ROWS), 1) < count[0]
    out_ref[...] = jnp.where(alive, result, jnp.zeros_like(result))

    for extra in (True, False):
        @pl.when(has_extra == extra)
        def _():
            sent = fit.at[pl.ds(0, 78 if extra else 79)]
            pltpu.make_async_copy(sent, sent, rs_send).wait()
            sent = fitted.at[pl.ds(0, 126 if extra else 63)]
            pltpu.make_async_copy(sent, sent, ag_send).wait()

    @pl.when(c == owner)
    def _():
        for many in (32, 31):
            sent = pieces.at[pl.ds(0, many)]
            pltpu.make_async_copy(sent, sent, d_send).wait()


def body(densities, tensor, metric, row_count):
    hbm = pl.BlockSpec(memory_space=pltpu.HBM)
    dma = pltpu.SemaphoreType.DMA
    bf16, f32 = jnp.bfloat16, jnp.float32
    out = pl.pallas_call(
        kernel,
        name="coulomb",
        out_shape=pltpu.VMEM((K // 2, ROWS), f32),
        in_specs=[hbm, hbm, hbm, hbm],
        out_specs=pl.BlockSpec(memory_space=pltpu.VMEM),
        scratch_shapes=[
            pltpu.SMEM((1,), jnp.int32),
            pltpu.VMEM((ROWS, AUX), bf16),
            pltpu.VMEM((COLS, AUX), bf16),
            pltpu.VMEM((AUX, ROWS), bf16),
            pltpu.VMEM((AUX, COLS), bf16),
            pltpu.VMEM((K, ROWS), bf16),
            pltpu.VMEM((128, K, TILE), bf16),
            pltpu.VMEM((128, K, TILE), bf16),
            pltpu.VMEM((2, K, TILE), bf16),
            pltpu.VMEM((128, K, TILE), bf16),
            pltpu.VMEM((2, K, COLS), f32),
            pltpu.VMEM((5, 8, TILE), bf16),
            pltpu.VMEM((32, 5, 8, TILE), bf16),
            pltpu.VMEM((2, K // 2, ROWS), f32),
            pltpu.VMEM((K // 2, ROWS), f32),
            dma, dma, dma((AUX // WIDTH,)), dma, dma, dma,
            dma, dma((4,)), dma, dma, dma, dma((4,)), dma, dma,
        ],
        compiler_params=pltpu.CompilerParams(
            collective_id=0, has_side_effects=True, vmem_limit_bytes=54 << 20
        ),
    )(row_count, densities, tensor, metric.T)
    return out.astype(bf16)


def solution(mesh):
    placed = (P(None, "pairs"), P("pairs", "aux"), P("aux", "pairs"), P("pairs"))
    return jax.shard_map(
        body, mesh=mesh, in_specs=placed, out_specs=P("aux", "pairs"), check_vma=False
    )
```
